32 devices in a mesh: ep: 8 (over z, y), dp: 4 (over x, core).
Axes of the slice: x: 2, y: 2, z: 4, core: 2. Of those that a mesh axis runs over, the one named last changes fastest.
Arguments:
- tokens: bfloat16 [4096, 3584], P(('ep', 'dp')), may hold values from -6 to 6
- cotangent: bfloat16 [4096, 3584], P(('ep', 'dp')), may hold values from -6 to 6
- routes: int32 [4096, 1], P(('ep', 'dp')), may hold values from 0 to 7; in each aligned block of 128 rows (0 to 127, 128 to 255, ...) at most 24 rows name the same one
- router_probs: float32 [4096, 1], P(('ep', 'dp')), may hold values from 0.1 to 1
- up_weight: bfloat16 [8, 3584, 1024], P('ep', None, 'dp'), may hold values from -0.09375 to 0.09375
- down_weight: bfloat16 [8, 1024, 3584], P('ep', 'dp'), may hold values from -0.1875 to 0.1875
- moving: int32 [4], replicated, may hold values 0 or 1
Outputs:
- outputs: bfloat16 [4096, 3584], P(('ep', 'dp'))
- input_grad: bfloat16 [4096, 3584], P(('ep', 'dp'))
- up_grad: bfloat16 [8, 3584, 1024], P('ep', None, 'dp')
- down_grad: bfloat16 [8, 1024, 3584], P('ep', 'dp')
The draws below stay inside these ranges and needn't reach their ends.
Inputs may be any that keep to these rules, and one draw needn't show every extreme that they name: `routes`: within each device's aligned block of 128 rows, no expert is named by more than 24 rows, a bound that some block reaches.
All inputs are finite; a program needn't handle non-finite values.
Results may differ from the reference program's by a relative error of at most 0.0095.
Values may be sent and summed in bfloat16 or wider, within the bound.
No kernel may reach another device: no remote copies, remote signals or barrier semaphores. Data moves between devices by JAX's collectives and lax.ppermute only.
A program may use at most 128 MiB of HBM per device.

```python
import math
import jax
import jax.numpy as jnp
import numpy as np
from jax import lax

D = 3584
HID = 1024
TOPK = 1
TOK_DEV = 128
EXPERTS = 8
CAP = 24
TOKENS = 4096
N_EP = 8
N_DP = 4


def place_ends(entries, stream_key, low, high):
    shape = entries.shape
    place = [jax.random.randint(jax.random.fold_in(stream_key, axis), (), 0, shape[axis]) for axis in range(len(shape))]
    entries = entries.at[tuple(place)].set(low)
    longest = shape.index(max(shape))
    place[longest] = (place[longest] + 1) % shape[longest]
    return entries.at[tuple(place)].set(high)


def block_levels(stream_key, extent, pieces, least, top_value):
    level, own = 1.0, jax.random.fold_in(stream_key, 6)
    for axis_at, shards_of in pieces:
        draws = jnp.exp(jax.random.uniform(jax.random.fold_in(own, axis_at), (shards_of,), jnp.float32, least / len(pieces), top_value / len(pieces)))
        level = level * jnp.repeat(draws, extent[axis_at] // shards_of).reshape([-1 if axis == axis_at else 1 for axis in range(len(extent))])
    return level


def assign_block(stream_key, own, number, rows, amount, top, most, lean):
    ranking = jax.random.permutation(stream_key, amount)
    heavy_load, usual = load_shares(amount, rows * top, most, lean, True), load_shares(amount, rows * top, most, lean, False)
    places = jnp.arange(amount)

    def named(tallies, rotation):
        used = int((tallies > 0).sum())
        fixed = max(1, used // 4)
        moved = fixed + (places - fixed + rotation * (used - fixed)) % max(1, amount - fixed)
        return jnp.zeros((amount,), jnp.int32).at[ranking[jnp.where(places < fixed, places, moved)]].set(jnp.asarray(tallies, jnp.int32))

    tallies = jnp.where(number % 4 == 0, named(heavy_load, number // 4), named(usual, number - number // 4 - 1))
    mixed = jax.random.permutation(jax.random.fold_in(own, 3), amount)
    giver, receiver = mixed[0:amount // 2 * 2:2], mixed[1:amount // 2 * 2:2]
    slack = jnp.minimum(tallies[giver] - 1, most - tallies[receiver]) // 2
    slack = jnp.where((giver == ranking[0]) | (receiver == ranking[0]) | (tallies[receiver] == 0), 0, jnp.maximum(slack, 0))
    moved = jax.random.randint(jax.random.fold_in(own, 4), (amount // 2,), 0, 1 << 20) % (slack + 1)
    tallies = tallies.at[giver].add(-moved).at[receiver].add(moved)
    labels = jnp.searchsorted(jnp.cumsum(tallies), jnp.arange(rows * top), side="right").astype(jnp.int32)
    listing = labels.reshape(top, rows).T
    listing = listing[jax.random.permutation(jax.random.fold_in(own, 1), rows)]
    rotation = jax.random.randint(jax.random.fold_in(own, 2), (rows, 1), 0, top)
    return jnp.take_along_axis(listing, (jnp.arange(top)[None, :] + rotation) % top, axis=1)


def load_shares(count, total, most, lean, full):
    portions = [(1 << 20) // math.isqrt(standing ** lean) + 1 for standing in range(1, count + 1)]
    largest = most if full else min(most, max(-(-total // count), total * portions[0] // sum(portions)))
    least = 1 if total - largest >= count - 1 else 0
    counts, surplus = [largest] + [least] * (count - 1), total - largest - least * (count - 1)
    while surplus > 0:
        free = [i for i in range(1, count) if counts[i] < largest] or [i for i in range(1, count) if counts[i] < most]
        whole, budget = sum([portions[i] for i in free]), surplus
        for i in free:
            extra = min(most - counts[i], max(1, budget * portions[i] // whole), surplus)
            counts[i] = counts[i] + extra
            surplus = surplus - extra
    return np.array(counts)


def centred(rng, dims, width, reach, cuts=(), held_as=jnp.bfloat16):
    gain = block_levels(rng, dims, cuts, -0.22, 0.18) if cuts else 1.0
    drawn = jax.random.normal(rng, dims, jnp.float32) * width * gain
    return jnp.minimum(jnp.maximum(drawn, -reach), reach).astype(held_as)


def setup_inputs(seed: int = 0) -> dict:
    keys = jax.random.split(jax.random.key(seed), 8)
    tokens = centred(keys[0], (TOKENS, D), 1.0, 6.0, ((0, 32),))
    cotangent = centred(keys[1], (TOKENS, D), 1.0, 6.0, ((0, 32),))
    routes_keys = jax.random.split(jax.random.fold_in(keys[2], 1), TOKENS // TOK_DEV)
    routes_turns = jax.random.permutation(jax.random.fold_in(keys[2], 3), TOKENS // TOK_DEV)
    routes = jax.vmap(lambda own, number: assign_block(jax.random.fold_in(keys[2], 2), own, number, TOK_DEV, EXPERTS, TOPK, CAP, 2))(routes_keys, routes_turns).reshape((TOKENS, TOPK))
    router_probs = jnp.clip(jnp.exp(math.log(1.0) - 2.3025851 * jax.random.uniform(keys[3], (TOKENS, TOPK), jnp.float32) ** block_levels(keys[3], (TOKENS, TOPK), ((0, 32),), -0.2, 0.2)), 0.1, 1.0)
    up_weight = centred(keys[4], (EXPERTS, D, HID), D ** -0.5, 0.09375, ((0, 8), (2, 4)))
    down_weight = centred(keys[5], (EXPERTS, HID, D), HID ** -0.5, 0.1875, ((0, 8), (1, 4)))
    moving = place_ends((jax.random.randint(keys[6], (EXPERTS // 2,), 0, 2) < 1).astype(jnp.int32), jax.random.fold_in(keys[6], 1), 0, 1)
    return dict(tokens=tokens, cotangent=cotangent, routes=routes, router_probs=router_probs, up_weight=up_weight, down_weight=down_weight, moving=moving)


def silu_grad(preact):
    sigmoid = jax.nn.sigmoid(preact)
    return sigmoid * (1.0 + preact * (1.0 - sigmoid))

def rounded_sum(parts):
    rounded = lax.optimization_barrier(parts.astype(jnp.bfloat16))
    return lax.optimization_barrier(jnp.sum(rounded.astype(jnp.float32), axis=0))

def reference(tokens, cotangent, routes, router_probs, up_weight, down_weight, moving):
    half_count = EXPERTS // 2
    buffer_rows = N_DP * N_EP * CAP
    hidden_share = HID // N_DP
    expert_of = routes[:, 0].astype(jnp.int32)
    router_weight = router_probs[:, 0]
    scaled_grad = (router_weight[:, None] * cotangent.astype(jnp.float32)).astype(jnp.bfloat16)
    one_hot = (expert_of[:, None] == jnp.arange(EXPERTS, dtype=jnp.int32)[None, :]).astype(jnp.int32)
    slot_rank = lax.optimization_barrier(jnp.sum(one_hot * (jnp.cumsum(one_hot, axis=0) - 1), axis=1)).astype(jnp.int32)
    token_ids = jnp.arange(TOKENS, dtype=jnp.int32)
    table = jnp.zeros((EXPERTS, buffer_rows), jnp.int32).at[expert_of, slot_rank].set(token_ids)
    filled = jnp.zeros((EXPERTS, buffer_rows), jnp.int32).at[expert_of, slot_rank].set(1)

    def one_expert(packed):
        up_matrix, down_matrix, picked, present = packed
        keep = present[:, None] == 1
        routed = jnp.where(keep, tokens[picked], jnp.zeros((), jnp.bfloat16))
        routed_grad = jnp.where(keep, scaled_grad[picked], jnp.zeros((), jnp.bfloat16))
        preact = jnp.dot(routed, up_matrix, preferred_element_type=jnp.float32)
        hidden = jax.nn.silu(preact).astype(jnp.bfloat16)
        hidden_split = hidden.astype(jnp.float32).reshape(buffer_rows, N_DP, hidden_share)
        down_split = down_matrix.astype(jnp.float32).reshape(N_DP, hidden_share, D)
        out_parts = jnp.einsum('rsh,shd->srd', hidden_split, down_split)
        expert_out = rounded_sum(out_parts).astype(jnp.bfloat16)
        hidden_grad = jnp.dot(routed_grad, down_matrix.T, preferred_element_type=jnp.float32)
        preact_grad = (hidden_grad * silu_grad(preact)).astype(jnp.bfloat16)
        grad_split = preact_grad.astype(jnp.float32).reshape(buffer_rows, N_DP, hidden_share)
        up_split = up_matrix.astype(jnp.float32).reshape(D, N_DP, hidden_share)
        input_parts = jnp.einsum('rsh,dsh->srd', grad_split, up_split)
        routed_input = rounded_sum(input_parts).astype(jnp.bfloat16)
        grad_up = jnp.dot(routed.T, preact_grad, preferred_element_type=jnp.float32).astype(jnp.bfloat16)
        grad_down = jnp.dot(hidden.T, routed_grad, preferred_element_type=jnp.float32).astype(jnp.bfloat16)
        return (expert_out, routed_input, grad_up, grad_down)
    expert_out, routed_input, grad_up, grad_down = lax.map(one_expert, (up_weight, down_weight, table, filled))
    mixed = expert_out[expert_of, slot_rank]
    outputs = (router_weight[:, None] * mixed.astype(jnp.float32)).astype(jnp.bfloat16)
    input_grad = routed_input[expert_of, slot_rank]
    device_ids = jnp.arange(EXPERTS, dtype=jnp.int32)
    pair_flag = moving[device_ids % half_count]
    partner = jnp.where(device_ids < half_count, device_ids + half_count, device_ids - half_count)
    held = jnp.where(pair_flag == 1, partner, device_ids).astype(jnp.int32)
    return (outputs, input_grad, grad_up[held], grad_down[held])
```

```python
import jax
import jax.numpy as jnp
from jax import lax
from jax.sharding import PartitionSpec as P

FEW_PEERS = 16


def swapped_by(value, axis, offset):
    return lax.ppermute(value, axis, [(i, i ^ offset) for i in range(lax.axis_size(axis))])


def gathered(value, axis):
    blocks = {0: value}
    bit = lax.axis_size(axis) // 2
    while bit:
        blocks.update({at ^ bit: swapped_by(block, axis, bit) for at, block in blocks.items()})
        bit //= 2
    return [blocks[at] for at in sorted(blocks)]


def exchanged(blocks, axis, first, count):
    if count <= FEW_PEERS:
        swaps = [swapped_by(blocks[first + k], axis, k) for k in range(1, count)]
        return [blocks[first]] + swaps
    group_ids = range(lax.axis_size(axis))
    groups = [group_ids[at : at + count] for at in range(0, len(group_ids), count)]
    places = jnp.arange(count) ^ (lax.axis_index(axis) % count)
    arrived = lax.all_to_all(
        blocks[first : first + count][places],
        axis,
        split_axis=0,
        concat_axis=0,
        axis_index_groups=[list(group) for group in groups],
        tiled=True,
    )[places]
    return [arrived[k] for k in range(count)]


def silu_grad(preact):
    sigmoid = jax.nn.sigmoid(preact)
    return sigmoid * (1.0 + preact * (1.0 - sigmoid))


def contract_rows(left, right):
    return lax.dot_general(
        left, right, (((0,), (0,)), ((), ())), preferred_element_type=jnp.float32
    )


def contract_cols(left, right):
    return lax.dot_general(
        left, right, (((1,), (1,)), ((), ())), preferred_element_type=jnp.float32
    )


def shards(tokens, cotangent, routes, router_probs, up_weight, down_weight, moving):
    ep_count = lax.axis_size("ep")
    dp_count = lax.axis_size("dp")
    half_count = ep_count // 2
    token_count, feature_count = tokens.shape
    capacity = 3 * token_count * routes.shape[1] // (2 * ep_count)
    slot_count = ep_count * capacity
    ep_index = lax.axis_index("ep")
    pair_ids = jnp.arange(half_count, dtype=jnp.int32)
    swapped = jnp.sum(jnp.where(pair_ids == ep_index % half_count, moving, 0)) == 1
    router_weight = router_probs[:, 0]

    def selection(expert_of):
        one_hot = (
            expert_of[:, None] == jnp.arange(ep_count, dtype=jnp.int32)[None, :]
        ).astype(jnp.int32)
        rank = jnp.sum(one_hot * (jnp.cumsum(one_hot, axis=0) - 1), axis=1)
        slot_of = (expert_of ^ ep_index) * capacity + rank
        return (jnp.arange(slot_count, dtype=jnp.int32)[:, None] == slot_of[None, :]).astype(
            jnp.bfloat16
        )

    def dispatched(select, rows):
        buffer = jnp.dot(select, rows, preferred_element_type=jnp.float32).astype(jnp.bfloat16)
        buffer = buffer.reshape(ep_count, capacity, feature_count)
        kept = exchanged(buffer, "ep", 0, half_count)
        other = exchanged(buffer, "ep", half_count, half_count)
        return kept, other

    scaled_grad = (router_weight[:, None] * cotangent.astype(jnp.float32)).astype(jnp.bfloat16)
    partner_routes = swapped_by(routes, "ep", half_count)
    partner_tokens = swapped_by(tokens, "ep", half_count)
    partner_grad = swapped_by(scaled_grad, "ep", half_count)
    ups = gathered(up_weight[0], "dp")
    downs = gathered(down_weight[0], "dp")
    select = selection(routes[:, 0])
    partner_select = selection(partner_routes[:, 0])
    kept_rows, other_rows = dispatched(select, tokens)
    kept_grad, other_grad = dispatched(select, scaled_grad)
    kept_rows_2, other_rows_2 = dispatched(partner_select, partner_tokens)
    kept_grad_2, other_grad_2 = dispatched(partner_select, partner_grad)
    routed = jnp.concatenate(kept_rows + kept_rows_2, axis=0)
    routed_grad = jnp.concatenate(kept_grad + kept_grad_2, axis=0)
    other_routed = jnp.concatenate(other_rows + other_rows_2, axis=0)
    other_routed_grad = jnp.concatenate(other_grad + other_grad_2, axis=0)

    hiddens, preact_grads = [], []
    out_sum = jnp.zeros((slot_count, feature_count), jnp.float32)
    input_sum = jnp.zeros((slot_count, feature_count), jnp.float32)
    for up_block, down_block in zip(ups, downs):
        preact = jnp.dot(routed, up_block, preferred_element_type=jnp.float32)
        hidden = jax.nn.silu(preact).astype(jnp.bfloat16)
        hidden_grad = contract_cols(routed_grad, down_block)
        preact_grad = (hidden_grad * silu_grad(preact)).astype(jnp.bfloat16)
        out_sum = out_sum + jnp.dot(hidden, down_block, preferred_element_type=jnp.float32)
        input_sum = input_sum + contract_cols(preact_grad, up_block)
        hiddens.append(hidden)
        preact_grads.append(preact_grad)

    def returned(total):
        blocks = total.astype(jnp.bfloat16).reshape(ep_count, capacity, feature_count)
        back = exchanged(blocks, "ep", 0, ep_count)
        return contract_rows(select, jnp.concatenate(back, axis=0))

    outputs = (router_weight[:, None] * returned(out_sum)).astype(jnp.bfloat16)
    input_grad = returned(input_sum).astype(jnp.bfloat16)

    local = jnp.stack(hiddens + preact_grads)
    remote = swapped_by(local, "ep", half_count)
    half_rows = slot_count // 2
    remote = jnp.concatenate([remote[:, half_rows:], remote[:, :half_rows]], axis=1)
    factors = jnp.where(swapped, remote, local)
    hidden_all = jnp.concatenate(
        [factors[0]] + [swapped_by(factors[k], "dp", k) for k in range(1, dp_count)], axis=0
    )
    preact_grad_all = jnp.concatenate(
        [factors[dp_count]]
        + [swapped_by(factors[dp_count + k], "dp", k) for k in range(1, dp_count)],
        axis=0,
    )
    routed_all = jnp.concatenate(gathered(jnp.where(swapped, other_routed, routed), "dp"), axis=0)
    routed_grad_all = jnp.concatenate(
        gathered(jnp.where(swapped, other_routed_grad, routed_grad), "dp"), axis=0
    )
    up_grad = contract_rows(routed_all, preact_grad_all).astype(jnp.bfloat16)[None]
    down_grad = contract_rows(hidden_all, routed_grad_all).astype(jnp.bfloat16)[None]
    return (outputs, input_grad, up_grad, down_grad)


def solution(mesh):
    in_specs = (
        P(("ep", "dp"), None),
        P(("ep", "dp"), None),
        P(("ep", "dp"), None),
        P(("ep", "dp"), None),
        P("ep", None, "dp"),
        P("ep", "dp", None),
        P(),
    )
    out_specs = (
        P(("ep", "dp"), None),
        P(("ep", "dp"), None),
        P("ep", None, "dp"),
        P("ep", "dp", None),
    )
    return jax.shard_map(shards, mesh=mesh, in_specs=in_specs, out_specs=out_specs, check_vma=False)
```
